32 devices in a mesh: context: 8 (over y, x, core), tensor: 4 (over z).
Axes of the slice: x: 2, y: 2, z: 4, core: 2. Of those that a mesh axis runs over, the one named last changes fastest.
Arguments:
- activations: bfloat16 [4096, 3072], P('context', 'tensor'), may hold values from -6 to 6
- qkv_weight: bfloat16 [3072, 3, 4096], P(None, None, 'tensor'), may hold values from -0.109375 to 0.109375
- log_decay: float32 [4096, 32], P('context', 'tensor'), may hold values from -1.5 to 0, as said below
- lengths: int32 [8], P('context'), may hold values from 256 to 512, as said below
- out_grad: bfloat16 [4096, 4096], P('context', 'tensor'), may hold values from -0.0014648438 to 0.0014648438
Outputs:
- weight_grad: float32 [3072, 3, 4096], P('context', None, 'tensor')
The draws below stay inside these ranges and needn't reach their ends.
Inputs may be any that keep to these rules, and one draw needn't show every extreme that they name: `log_decay`: Negative; entries vary from token to token. `lengths`: each entry is a multiple of 256; the live tokens are the first slots of their shard; in every draw at least one shard is full.
All inputs are finite; a program needn't handle non-finite values.
Results may differ from the reference program's by a relative error of at most 0.015.
Values may be sent and summed in bfloat16 or wider, within the bound.
A program may use at most 128 MiB of HBM per device.

```python
import math
import jax
import jax.numpy as jnp
from jax import lax

D = 3072
HEAD = 128
BLOCK = 256
TOK_DEV = 512
HEAD_COUNT = 32
TOKEN_SLOTS = 4096


def draw_log_decay(key, part):
    random_seed_keys = jax.random.split(jax.random.fold_in(key, 17), 7)
    shard_count = TOKEN_SLOTS // TOK_DEV
    fast_share = 0.5
    is_fast = jax.random.uniform(random_seed_keys[0], (HEAD_COUNT,)) < fast_share
    fast_rate = jnp.exp(jax.random.uniform(random_seed_keys[1], (HEAD_COUNT,), minval=math.log(1.0 / 50.0), maxval=math.log(1.0 / 30.0)))
    slow_rate = jnp.exp(jax.random.uniform(random_seed_keys[2], (HEAD_COUNT,), minval=math.log(0.1), maxval=math.log(0.3))) / TOKEN_SLOTS
    head_rate = jnp.where(is_fast, fast_rate, slow_rate)
    shard_factor = jnp.exp(jax.random.uniform(random_seed_keys[3], (shard_count, HEAD_COUNT), minval=math.log(0.5), maxval=math.log(2.0)))
    token_factor = jax.random.uniform(random_seed_keys[4], (TOKEN_SLOTS, HEAD_COUNT), minval=0.7, maxval=1.4)
    baseline_decay_rate = jnp.repeat(shard_factor, TOK_DEV, axis=0) * token_factor * head_rate[None, :]
    flurry_location = jax.random.randint(random_seed_keys[5], (2,), 0, TOKEN_SLOTS)
    flurry_depth = -jnp.log(1.0 - jax.random.uniform(random_seed_keys[6], (2, HEAD_COUNT), minval=0.2, maxval=0.5))
    token_position = jnp.arange(TOKEN_SLOTS)
    flurry_list = jnp.sum((token_position[:, None, None] == flurry_location[None, :, None]) * flurry_depth[None], axis=1)
    return (-(baseline_decay_rate + flurry_list)).astype(jnp.float32)


def draw_lengths(key, part):
    random_seed_keys = jax.random.split(jax.random.fold_in(key, 29), 2)
    shard_count = TOKEN_SLOTS // TOK_DEV
    block_count = TOK_DEV // BLOCK
    block_live = jax.random.randint(random_seed_keys[0], (shard_count,), 1, block_count + 1)
    full_shard = jax.random.randint(random_seed_keys[1], (), 0, shard_count)
    block_live = jnp.where(jnp.arange(shard_count) == full_shard, block_count, block_live)
    return (block_live * BLOCK).astype(jnp.int32)


def with_spikes(values, own_key, source, target, shards_of, factor):
    owner, partner = [(jnp.arange(values.shape[position]) // (values.shape[position] // shards_of)).reshape([-1 if axis == position else 1 for axis in range(values.ndim)]) for position in (source, target)]
    chosen = jax.random.permutation(own_key, shards_of)[partner]
    strong = (owner == chosen) | (owner == (partner + shards_of // 2) % shards_of)
    return jnp.where(strong, factor * values, values)


def steps_of(rng, extent, pieces, low, largest):
    gain, own = 1.0, jax.random.fold_in(rng, 6)
    for axis_at, shards_of in pieces:
        steps = jnp.exp(jax.random.uniform(jax.random.fold_in(own, axis_at), (shards_of,), jnp.float32, low / len(pieces), largest / len(pieces)))
        gain = gain * jnp.repeat(steps, extent[axis_at] // shards_of).reshape([-1 if axis == axis_at else 1 for axis in range(len(extent))])
    return gain


def gaussian(key, shape, width, reach, pieces=(), held_as=jnp.bfloat16):
    array = width * jax.random.normal(key, shape, jnp.float32)
    if pieces:
        array = array * steps_of(key, shape, pieces, -0.22, 0.18)
    return jnp.clip(array, -reach, reach).astype(held_as)


def gaussian_with(stream_key, shape, width, most, cuts, heavy, kind=jnp.bfloat16):
    values = width * jax.random.normal(stream_key, shape, jnp.float32)
    if cuts:
        values = values * steps_of(stream_key, shape, cuts, -0.22, 0.18)
    return jnp.clip(with_spikes(values, jax.random.fold_in(stream_key, 3), *heavy), -most, most).astype(kind)


def setup_inputs(seed: int = 0) -> dict:
    splits = jax.random.split(jax.random.key(seed), 6)
    activations = gaussian_with(splits[0], (TOKEN_SLOTS, D), 1.0, 6.0, ((0, 8), (1, 4)), (0, 1, 8, 2.0))
    qkv_weight = gaussian(splits[1], (D, 3, HEAD_COUNT * HEAD), D ** -0.5, 0.109375, ((2, 4),))
    log_decay = draw_log_decay(jax.random.fold_in(splits[5], 71), 0)
    lengths = draw_lengths(jax.random.fold_in(splits[5], 71), 0)
    out_grad = gaussian(splits[4], (TOKEN_SLOTS, HEAD_COUNT * HEAD), (1.0 / TOKEN_SLOTS), 0.0014648438, ((0, 8), (1, 4)))
    return {"activations": activations, "qkv_weight": qkv_weight, "log_decay": log_decay, "lengths": lengths, "out_grad": out_grad}


def rounded(value):
    return lax.optimization_barrier(value.astype(jnp.bfloat16)).astype(jnp.float32)


def shard_sums(query, key_matrix_rows, value_matrix_rows, output_gradient, decays):
    run_sum = jnp.cumsum(decays, axis=0)
    shard_sum = run_sum[-1]
    score_scale_factor = HEAD ** -0.5
    until_finish = jnp.exp(shard_sum[None, :] - run_sum)
    decayed_key_rows = rounded(key_matrix_rows.astype(jnp.float32) * until_finish[:, :, None])
    partition_state = jnp.einsum("jla,jlu->lau", decayed_key_rows, value_matrix_rows.astype(jnp.float32)).astype(jnp.bfloat16)
    decayed_query_rows = rounded(query.astype(jnp.float32) * (score_scale_factor * jnp.exp(run_sum))[:, :, None])
    state_gradient = jnp.einsum("jla,jlu->lau", decayed_query_rows, output_gradient.astype(jnp.float32)).astype(jnp.bfloat16)
    return partition_state, state_gradient, shard_sum.astype(jnp.bfloat16)


def shard_grads(query, key_matrix_rows, value_matrix_rows, output_gradient, decays, is_live, incoming, from_later):
    run_sum = jnp.cumsum(decays, axis=0)
    shard_sum = run_sum[-1]
    score_scale_factor = HEAD ** -0.5
    token_position = jnp.arange(TOK_DEV, dtype=jnp.int32)
    causal = token_position[:, None] >= token_position[None, :]
    gap_matrix = run_sum.T[:, :, None] - run_sum.T[:, None, :]
    decay_matrix = jnp.exp(jnp.where(causal[None], gap_matrix, -jnp.inf))
    query_wide_float = query.astype(jnp.float32)
    key_wide_float = key_matrix_rows.astype(jnp.float32)
    value_wide_float = value_matrix_rows.astype(jnp.float32)
    gradient_wide_float = output_gradient.astype(jnp.float32)
    probability_wide_float = rounded(jnp.einsum("thd,shd->hts", query_wide_float, key_wide_float) * score_scale_factor * decay_matrix)
    score_wide_float = rounded(jnp.einsum("thd,shd->hts", gradient_wide_float, value_wide_float) * decay_matrix)
    arriving_wide_float = rounded(incoming)
    subsequent_wide_float = rounded(from_later)
    since_beginning = jnp.exp(run_sum)[:, :, None]
    until_finish = jnp.exp(shard_sum[None, :] - run_sum)[:, :, None]
    query_gradient = score_scale_factor * (jnp.einsum("zmb,bzw->mzw", score_wide_float, key_wide_float) + since_beginning * jnp.einsum("bzf,zof->bzo", gradient_wide_float, arriving_wide_float))
    key_gradient = score_scale_factor * jnp.einsum("rvz,vrj->zrj", score_wide_float, query_wide_float) + until_finish * jnp.einsum("bzf,zof->bzo", value_wide_float, subsequent_wide_float)
    value_gradient = jnp.einsum("rvz,vrj->zrj", probability_wide_float, gradient_wide_float) + until_finish * jnp.einsum("cnf,nfg->cng", key_wide_float, subsequent_wide_float)
    stacked = jnp.stack([query_gradient, key_gradient, value_gradient], axis=1) * is_live[:, None, None, None]
    return stacked.astype(jnp.bfloat16).reshape(TOK_DEV, 3 * HEAD_COUNT * HEAD)


def decay_step(running, shard_item):
    partition_state, shard_total = shard_item
    updated = jnp.exp(shard_total.astype(jnp.float32))[:, None, None] * running + partition_state.astype(jnp.float32)
    return updated, running


def reference(activations, qkv_weight, log_decay, lengths, out_grad):
    shards = TOKEN_SLOTS // TOK_DEV
    col_width = HEAD_COUNT * HEAD
    token_position = jnp.arange(TOKEN_SLOTS, dtype=jnp.int32)
    is_live = (token_position % TOK_DEV < jnp.repeat(lengths, TOK_DEV)).astype(jnp.float32)
    projected = jnp.dot(activations, qkv_weight.reshape(D, 3 * col_width), preferred_element_type=jnp.float32).astype(jnp.bfloat16)
    projected = (projected * is_live.astype(jnp.bfloat16)[:, None]).reshape(shards, TOK_DEV, 3, HEAD_COUNT, HEAD)
    output_gradient = out_grad.reshape(shards, TOK_DEV, HEAD_COUNT, HEAD)
    decays = (log_decay * is_live[:, None]).reshape(shards, TOK_DEV, HEAD_COUNT)
    live_shards = is_live.reshape(shards, TOK_DEV)
    input_shards = activations.reshape(shards, TOK_DEV, D)
    states, grad_states, totals = lax.map(lambda shard_item: shard_sums(shard_item[0][:, 0], shard_item[0][:, 1], shard_item[0][:, 2], shard_item[1], shard_item[2]), (projected, output_gradient, decays))
    start_state = jnp.zeros((HEAD_COUNT, HEAD, HEAD), jnp.float32)
    _, incoming = lax.scan(decay_step, start_state, (states, totals))
    _, from_later = lax.scan(decay_step, start_state, (grad_states, totals), reverse=True)

    def grads_step(running, shard_item):
        input_shard, qkv_shard, grad_shard, decay_shard, live_shard, incoming_shard, later_shard = shard_item
        qkv_grad = shard_grads(qkv_shard[:, 0], qkv_shard[:, 1], qkv_shard[:, 2], grad_shard, decay_shard, live_shard, incoming_shard, later_shard)
        partial_grad = jnp.dot(input_shard.T, qkv_grad, preferred_element_type=jnp.float32).astype(jnp.bfloat16)
        return running + partial_grad.astype(jnp.float32), None

    start_grad = jnp.zeros((D, 3 * col_width), jnp.float32)
    weight_grad, _ = lax.scan(grads_step, start_grad, (input_shards, projected, output_gradient, decays, live_shards, incoming, from_later))
    return weight_grad.reshape(D, 3, col_width)
```

```python
import functools

import jax
import jax.numpy as jnp
from jax import lax
from jax.experimental import pallas as pl
from jax.experimental.pallas import tpu as pltpu
from jax.sharding import PartitionSpec as P


F32 = jnp.float32
BF16 = jnp.bfloat16


def contract(a, b, dims):
    return lax.dot_general(a, b, (dims, ((), ())), preferred_element_type=F32)


ROWS = ((0,), (0,))
LANES = ((1,), (1,))
PLAIN = ((1,), (0,))


def states_kernel(scale, q_ref, k_ref, v_ref, g_ref, c_ref, state_ref, grad_ref):
    c = c_ref[...]
    total = c[-1:, :]
    weighted_k = (k_ref[...].astype(F32) * jnp.exp(total - c)).astype(BF16)
    state_ref[0] = contract(weighted_k, v_ref[...], ROWS).astype(BF16)
    weighted_q = (q_ref[...].astype(F32) * (scale * jnp.exp(c))).astype(BF16)
    grad_ref[0] = contract(weighted_q, g_ref[...], ROWS).astype(BF16)


def intra_kernel(scale, q_ref, k_ref, v_ref, g_ref, c_ref, ct_ref, dq_ref, dk_ref, dv_ref):
    head = pl.program_id(0)
    q, k, v, g = q_ref[...], k_ref[...], v_ref[...], g_ref[...]
    tokens, width = q.shape
    column = jnp.concatenate([c_ref[...]] * (tokens // width), axis=1)
    gap = column - ct_ref[pl.ds(head, 1), :]
    row_at = lax.broadcasted_iota(jnp.int32, (tokens, tokens), 0)
    col_at = lax.broadcasted_iota(jnp.int32, (tokens, tokens), 1)
    decay = jnp.exp(jnp.where(row_at >= col_at, gap, -jnp.inf))
    prob = (contract(q, k, LANES) * scale * decay).astype(BF16)
    score = (contract(g, v, LANES) * decay).astype(BF16)
    dq_ref[...] = scale * contract(score, k, PLAIN)
    dk_ref[...] = scale * contract(score, q, ROWS)
    dv_ref[...] = contract(prob, g, ROWS)


def inter_kernel(scale, len_ref, k_ref, v_ref, g_ref, c_ref, in_ref, later_ref, dq_ref, dk_ref, dv_ref,
                 oq_ref, ok_ref, ov_ref):
    c = c_ref[...]
    live = lax.broadcasted_iota(jnp.int32, c.shape, 0) < len_ref[0]
    until = jnp.exp(c[-1:, :] - c)
    dq = dq_ref[...] + scale * jnp.exp(c) * contract(g_ref[...], in_ref[0], LANES)
    dk = dk_ref[...] + until * contract(v_ref[...], later_ref[0], LANES)
    dv = dv_ref[...] + until * contract(k_ref[...], later_ref[0], PLAIN)
    oq_ref[...] = jnp.where(live, dq, 0.0).astype(BF16)
    ok_ref[...] = jnp.where(live, dk, 0.0).astype(BF16)
    ov_ref[...] = jnp.where(live, dv, 0.0).astype(BF16)


def swap(value, size, distance):
    return lax.ppermute(value, "context", [(i, i ^ distance) for i in range(size)])


def gather_features(activations, weight, columns):
    size = lax.axis_size("tensor")
    me = lax.axis_index("tensor")
    depth = activations.shape[1]

    def product(chunk, owner):
        rows = lax.dynamic_slice_in_dim(weight, owner * depth, depth, 0)
        return [jnp.dot(chunk, rows[:, part], preferred_element_type=F32) for part in range(3)]

    if size != 4:
        every = lax.all_gather(activations, "tensor", axis=0)
        sums = None
        for owner in range(size):
            terms = product(every[owner], owner)
            sums = terms if sums is None else [a + b for a, b in zip(sums, terms)]
        return every, sums
    up = [(i, i + 1) for i in range(size - 1)]
    down = [(i + 1, i) for i in range(size - 1)]
    from_low, from_high = [activations], [activations]
    for _ in range(size - 1):
        from_low.append(lax.ppermute(from_low[-1], "tensor", up))
        from_high.append(lax.ppermute(from_high[-1], "tensor", down))
    first, last = me == 0, me == size - 1
    chunks = [
        (activations, me),
        (jnp.where(first, from_high[1], from_low[1]), jnp.where(first, 1, me - 1)),
        (jnp.where(me < 2, from_high[2], from_low[2]), jnp.where(me < 2, me + 2, me - 2)),
        (
            jnp.where(first, from_high[3], jnp.where(last, from_low[3], from_high[1])),
            jnp.where(first, 3, jnp.where(last, 0, me + 1)),
        ),
    ]
    every = jnp.zeros((size,) + activations.shape, BF16)
    sums = None
    for chunk, owner in chunks:
        every = lax.dynamic_update_slice(every, chunk[None], (owner, 0, 0))
        terms = product(chunk, owner)
        sums = terms if sums is None else [a + b for a, b in zip(sums, terms)]
        sums = list(lax.optimization_barrier(tuple(sums)))
    return every, sums


def scatter_sum(lhs, rhs, bits, me, size):
    count = lhs.ndim - 2

    def pick(value, bit, mine):
        at = (me >> (bit + 1)) & 1
        return lax.dynamic_index_in_dim(value, at if mine else 1 - at, count - 1 - bit, keepdims=True)

    def times(block):
        flat = block.reshape(-1, block.shape[-1])
        return jnp.dot(flat, rhs, preferred_element_type=F32).reshape(block.shape[:-1] + (rhs.shape[1],))

    received = []
    keep = lhs
    for bit in bits:
        send = times(pick(keep, bit, False))
        for value in received:
            send = send + pick(value, bit, False).astype(F32)
        keep = pick(keep, bit, True)
        received = [pick(value, bit, True) for value in received]
        received.append(swap(send.astype(BF16), size, 2 << bit))
    total = times(keep)
    for value in received:
        total = total + value.astype(F32)
    return total.reshape(lhs.shape[-2], rhs.shape[1])


def shards(activations, qkv_weight, log_decay, lengths, out_grad):
    size = lax.axis_size("context")
    me = lax.axis_index("context")
    core = me & 1
    chip = me >> 1
    chips = size // 2
    tokens = activations.shape[0]
    heads = log_decay.shape[1]
    columns = out_grad.shape[1]
    width = columns // heads
    half = heads // 2
    scale = width ** -0.5

    token_at = jnp.arange(tokens, dtype=jnp.int32)
    live = token_at < lengths[0]
    run_sum = jnp.cumsum(log_decay * live.astype(F32)[:, None], axis=0)
    run_wide = jnp.repeat(run_sum, width, axis=1)
    run_rows = run_sum.T
    own_total = run_sum[-1].astype(BF16).astype(F32)
    totals = jnp.where(jnp.arange(size)[:, None] == me, own_total[None], 0.0)
    distance = 1
    while distance < size:
        totals = totals + swap(totals, size, distance)
        distance *= 2

    every, sums = gather_features(activations, qkv_weight, columns)
    q, k, v = [jnp.where(live[:, None], s, 0.0).astype(BF16) for s in sums]

    rows = qkv_weight.shape[0] // size
    features = every.transpose(0, 2, 1).reshape(chips, 2, rows, tokens)
    own_rows = lax.dynamic_index_in_dim(features, core, 1, keepdims=False)
    other_rows = swap(lax.dynamic_index_in_dim(features, 1 - core, 1, keepdims=False), size, 1)
    lhs = jnp.concatenate([own_rows, other_rows], axis=2)

    head_spec = pl.BlockSpec((tokens, width), lambda h: (0, h))
    square_spec = pl.BlockSpec((1, width, width), lambda h: (h, 0, 0))
    wide = lambda kind: jax.ShapeDtypeStruct((tokens, columns), kind)
    squares = jax.ShapeDtypeStruct((heads, width, width), BF16)
    state, grad_state = pl.pallas_call(
        functools.partial(states_kernel, scale),
        grid=(heads,),
        in_specs=[head_spec] * 5,
        out_specs=[square_spec] * 2,
        out_shape=[squares] * 2,
        cost_estimate=pl.CostEstimate(flops=4 * tokens * columns * width, bytes_accessed=12 * tokens * columns, transcendentals=0),
        name="states",
    )(q, k, v, out_grad, run_wide)

    both = jnp.stack([state, grad_state])
    other = swap(both, size, 1)
    mine_half = lax.dynamic_slice_in_dim(both, core * half, half, 1).astype(F32)
    other_half = lax.dynamic_slice_in_dim(other, core * half, half, 1).astype(F32)
    pair_totals = lax.dynamic_slice_in_dim(totals, chip * 2, 2, 0)
    pair_half = lax.dynamic_slice_in_dim(pair_totals, core * half, half, 1)
    low, high = [jnp.where(core == which, mine_half, other_half) for which in (0, 1)]
    chip_state = (jnp.exp(pair_half[1])[:, None, None] * low[0] + high[0]).astype(BF16)
    chip_grad = (low[1] + jnp.exp(pair_half[0])[:, None, None] * high[1]).astype(BF16)

    upto = jnp.cumsum(totals, axis=0)
    totals_half = lax.dynamic_slice_in_dim(totals, core * half, half, 1)
    upto_half = lax.dynamic_slice_in_dim(upto, core * half, half, 1)
    chip_before = lax.dynamic_index_in_dim(upto_half - totals_half, chip * 2, 0, keepdims=False)
    chip_upto = lax.dynamic_index_in_dim(upto_half, chip * 2 + 1, 0, keepdims=False)
    incoming = jnp.zeros((half, width, width), F32)
    later = jnp.zeros((half, width, width), F32)
    for step in range(1, chips):
        peer = chip ^ step
        goes_up = peer > chip
        arrived = swap(jnp.where(goes_up, chip_state, chip_grad), size, 2 * step).astype(F32)
        peer_upto = lax.dynamic_index_in_dim(upto_half, peer * 2 + 1, 0, keepdims=False)
        peer_before = lax.dynamic_index_in_dim(upto_half - totals_half, peer * 2, 0, keepdims=False)
        gap = jnp.where(goes_up, peer_before - chip_upto, chip_before - peer_upto)
        term = jnp.exp(gap)[:, None, None] * arrived
        incoming = incoming + jnp.where(goes_up, 0.0, term)
        later = later + jnp.where(goes_up, term, 0.0)
    from_chips = jnp.stack([incoming, later]).astype(BF16)
    other_chips = swap(from_chips, size, 1)
    is_low = core == 0
    from_chips = jnp.concatenate(
        [jnp.where(is_low, from_chips, other_chips), jnp.where(is_low, other_chips, from_chips)], axis=1
    ).astype(F32)
    incoming = jnp.where(
        is_low, from_chips[0], jnp.exp(pair_totals[0])[:, None, None] * from_chips[0] + other[0].astype(F32)
    ).astype(BF16)
    later = jnp.where(
        is_low, jnp.exp(pair_totals[1])[:, None, None] * from_chips[1] + other[1].astype(F32), from_chips[1]
    ).astype(BF16)

    dq, dk, dv = pl.pallas_call(
        functools.partial(intra_kernel, scale),
        grid=(heads,),
        in_specs=[head_spec] * 5 + [pl.BlockSpec((heads, tokens), lambda h: (0, 0))],
        out_specs=[head_spec] * 3,
        out_shape=[wide(F32)] * 3,
        cost_estimate=pl.CostEstimate(
            flops=10 * tokens * tokens * columns, bytes_accessed=24 * tokens * columns, transcendentals=heads * tokens * tokens
        ),
        name="intra",
    )(q, k, v, out_grad, run_wide, run_rows)

    grads = pl.pallas_call(
        functools.partial(inter_kernel, scale),
        grid=(heads,),
        in_specs=[pl.BlockSpec(memory_space=pltpu.SMEM)] + [head_spec] * 4 + [square_spec] * 2 + [head_spec] * 3,
        out_specs=[head_spec] * 3,
        out_shape=[wide(BF16)] * 3,
        cost_estimate=pl.CostEstimate(flops=6 * tokens * columns * width, bytes_accessed=28 * tokens * columns, transcendentals=0),
        name="inter",
    )(lengths, k, v, out_grad, run_wide, incoming, later, dq, dk, dv)

    depth = chips.bit_length() - 1
    lhs = lhs.reshape((2,) * depth + lhs.shape[1:])
    results = []
    for part in grads:
        rhs = jnp.concatenate([part, swap(part, size, 1)], axis=0)
        orders = (tuple(range(depth)), tuple(reversed(range(depth))))
        piece = columns // 2
        results.append(
            jnp.concatenate(
                [
                    scatter_sum(lhs, rhs[:, at * piece : (at + 1) * piece], order, me, size)
                    for at, order in enumerate(orders)
                ],
                axis=1,
            )
        )
    return jnp.stack(results, axis=1)


def solution(mesh):
    return jax.shard_map(
        shards,
        mesh=mesh,
        in_specs=(
            P("context", "tensor"),
            P(None, None, "tensor"),
            P("context", "tensor"),
            P("context"),
            P("context", "tensor"),
        ),
        out_specs=P("context", None, "tensor"),
        check_vma=False,
    )
```

```python
import functools

import jax
import jax.numpy as jnp
from jax import lax
from jax.experimental import pallas as pl
from jax.experimental.pallas import tpu as pltpu
from jax.sharding import PartitionSpec as P


F32 = jnp.float32
BF16 = jnp.bfloat16


def contract(a, b, dims):
    return lax.dot_general(a, b, (dims, ((), ())), preferred_element_type=F32)


ROWS = ((0,), (0,))
LANES = ((1,), (1,))
PLAIN = ((1,), (0,))


def states_kernel(scale, q_ref, k_ref, v_ref, g_ref, c_ref, state_ref, grad_ref):
    c = c_ref[...]
    total = c[-1:, :]
    weighted_k = (k_ref[...].astype(F32) * jnp.exp(total - c)).astype(BF16)
    state_ref[0] = contract(weighted_k, v_ref[...], ROWS).astype(BF16)
    weighted_q = (q_ref[...].astype(F32) * (scale * jnp.exp(c))).astype(BF16)
    grad_ref[0] = contract(weighted_q, g_ref[...], ROWS).astype(BF16)


def intra_kernel(scale, q_ref, k_ref, v_ref, g_ref, c_ref, ct_ref, dq_ref, dk_ref, dv_ref):
    head = pl.program_id(0)
    q, k, v, g = q_ref[...], k_ref[...], v_ref[...], g_ref[...]
    tokens, width = q.shape
    column = jnp.concatenate([c_ref[...]] * (tokens // width), axis=1)
    gap = column - ct_ref[pl.ds(head, 1), :]
    row_at = lax.broadcasted_iota(jnp.int32, (tokens, tokens), 0)
    col_at = lax.broadcasted_iota(jnp.int32, (tokens, tokens), 1)
    decay = jnp.exp(jnp.where(row_at >= col_at, gap, -jnp.inf))
    prob = (contract(q, k, LANES) * scale * decay).astype(BF16)
    score = (contract(g, v, LANES) * decay).astype(BF16)
    dq_ref[...] = scale * contract(score, k, PLAIN)
    dk_ref[...] = scale * contract(score, q, ROWS)
    dv_ref[...] = contract(prob, g, ROWS)


def inter_kernel(scale, len_ref, k_ref, v_ref, g_ref, c_ref, in_ref, later_ref, dq_ref, dk_ref, dv_ref,
                 oq_ref, ok_ref, ov_ref):
    c = c_ref[...]
    live = lax.broadcasted_iota(jnp.int32, c.shape, 0) < len_ref[0]
    until = jnp.exp(c[-1:, :] - c)
    dq = dq_ref[...] + scale * jnp.exp(c) * contract(g_ref[...], in_ref[0], LANES)
    dk = dk_ref[...] + until * contract(v_ref[...], later_ref[0], LANES)
    dv = dv_ref[...] + until * contract(k_ref[...], later_ref[0], PLAIN)
    oq_ref[...] = jnp.where(live, dq, 0.0).astype(BF16)
    ok_ref[...] = jnp.where(live, dk, 0.0).astype(BF16)
    ov_ref[...] = jnp.where(live, dv, 0.0).astype(BF16)


def swap(value, size, distance):
    return lax.ppermute(value, "context", [(i, i ^ distance) for i in range(size)])


PIECES = 2
TILE = 256


def project_kernel(act_ref, live_ref, total_ref, weight_ref, every_ref, q_ref, k_ref, v_ref, totals_ref,
                   weights, sums, own_sem, weight_sem, send_sem, recv_sem, total_send, total_recv):
    size, me = lax.axis_size("tensor"), lax.axis_index("tensor")
    shard_count, shard = lax.axis_size("context"), lax.axis_index("context")
    depth = act_ref.shape[1]
    piece = act_ref.shape[0] // PIECES
    columns = q_ref.shape[1]
    tiles = columns // TILE

    def load(owner, part):
        rows = pl.ds(pl.multiple_of(owner * depth, depth), depth)
        return pltpu.make_async_copy(weight_ref.at[part, rows], weights.at[owner, part], weight_sem.at[owner, part])

    for at in range(size):
        owner = lax.rem(me + at, size)
        for part in range(3):
            load(owner, part).start()

    barrier = pltpu.get_barrier_semaphore()
    for target in (me - 1, me + 1):
        @pl.when((target >= 0) & (target < size))
        def _():
            pl.semaphore_signal(barrier, inc=1, device_id={"tensor": target}, device_id_type=pl.DeviceIdType.MESH)

    @pl.loop(1, shard_count)
    def _(step):
        peer = lax.rem(shard + step, shard_count)
        pl.semaphore_signal(barrier, inc=1, device_id={"context": peer}, device_id_type=pl.DeviceIdType.MESH)

    neighbours = jnp.where(me > 0, 1, 0) + jnp.where(me < size - 1, 1, 0)
    pl.semaphore_wait(barrier, neighbours + shard_count - 1)

    def rows_of(at):
        return pl.ds(pl.multiple_of(at * piece, piece), piece)

    def send(source, owner, at, side):
        return pltpu.make_async_remote_copy(
            src_ref=source,
            dst_ref=every_ref.at[owner, rows_of(at)],
            send_sem=send_sem.at[side, owner, at],
            recv_sem=recv_sem.at[owner, at],
            device_id={"tensor": me + 1 - 2 * side},
            device_id_type=pl.DeviceIdType.MESH,
        )

    def has_target(side):
        target = me + 1 - 2 * side
        return (target >= 0) & (target < size)

    def send_total(step):
        peer = lax.rem(shard + step, shard_count)
        return pltpu.make_async_remote_copy(
            src_ref=total_ref,
            dst_ref=totals_ref.at[shard],
            send_sem=total_send.at[peer],
            recv_sem=total_recv.at[shard],
            device_id={"context": peer},
            device_id_type=pl.DeviceIdType.MESH,
        )

    for at in range(PIECES):
        for side in range(2):
            @pl.when(has_target(side))
            def _():
                send(act_ref.at[rows_of(at)], me, at, side).start()

    @pl.loop(1, shard_count)
    def _(step):
        send_total(step).start()

    own = pltpu.make_async_copy(act_ref, every_ref.at[me], own_sem)
    own.start()
    totals_ref[shard] = total_ref[...]

    for part in range(3):
        load(me, part).wait()

    @pl.loop(0, 3 * tiles)
    def _(tile):
        part = tile // tiles
        cols = pl.ds(pl.multiple_of(lax.rem(tile, tiles) * TILE, TILE), TILE)
        sums[part, :, cols] = jnp.dot(act_ref[...], weights[me, part, :, cols], preferred_element_type=F32)

    own.wait()
    for distance in range(1, size):
        for side in range(2):
            owner = me + (2 * side - 1) * distance

            @pl.when((owner >= 0) & (owner < size))
            def _():
                for part in range(3):
                    load(owner, part).wait()

        @pl.loop(0, PIECES)
        def _(at):
            for side in range(2):
                owner = me + (2 * side - 1) * distance

                @pl.when((owner >= 0) & (owner < size))
                def _():
                    pltpu.make_async_copy(
                        every_ref.at[owner, rows_of(at)], every_ref.at[owner, rows_of(at)], recv_sem.at[owner, at]
                    ).wait()

                    @pl.when(has_target(side))
                    def _():
                        send(every_ref.at[owner, rows_of(at)], owner, at, side).start()

            @pl.loop(0, 2)
            def _(side):
                owner = me + (2 * side - 1) * distance

                @pl.when((owner >= 0) & (owner < size))
                def _():
                    @pl.loop(0, 3 * tiles)
                    def _(tile):
                        part = tile // tiles
                        cols = pl.ds(pl.multiple_of(lax.rem(tile, tiles) * TILE, TILE), TILE)
                        sums[part, rows_of(at), cols] += jnp.dot(
                            every_ref[owner, rows_of(at), :], weights[owner, part, :, cols], preferred_element_type=F32
                        )

    live = live_ref[...]
    for part, ref in enumerate((q_ref, k_ref, v_ref)):
        @pl.loop(0, tiles)
        def _(tile):
            cols = pl.ds(pl.multiple_of(tile * TILE, TILE), TILE)
            ref[:, cols] = (sums[part, :, cols] * live).astype(BF16)

    for side in range(2):
        @pl.when(has_target(side))
        def _():
            for distance in range(size):
                owner = me + (2 * side - 1) * distance

                @pl.when((owner >= 0) & (owner < size))
                def _():
                    for at in range(PIECES):
                        send(every_ref.at[owner, rows_of(at)], owner, at, side).wait_send()

    @pl.loop(1, shard_count)
    def _(step):
        peer = lax.rem(shard + step, shard_count)
        send_total(step).wait_send()
        pltpu.make_async_copy(total_ref, totals_ref.at[peer], total_recv.at[peer]).wait()


def project(activations, weight, live, total, shard_count, size):
    tokens, depth = activations.shape
    columns = weight.shape[2]
    vmem = pl.BlockSpec(memory_space=pltpu.VMEM)
    heads_out = [jax.ShapeDtypeStruct((tokens, columns), BF16)] * 3
    return pl.pallas_call(
        project_kernel,
        in_specs=[vmem] * 3 + [pl.BlockSpec(memory_space=pl.ANY)],
        out_specs=[vmem] * 5,
        out_shape=[jax.ShapeDtypeStruct((size, tokens, depth), BF16)]
        + heads_out
        + [jax.ShapeDtypeStruct((shard_count,) + total.shape, F32)],
        scratch_shapes=[
            pltpu.VMEM((size, 3, depth, columns), BF16),
            pltpu.VMEM((3, tokens, columns), F32),
            pltpu.SemaphoreType.DMA,
            pltpu.SemaphoreType.DMA((size, 3)),
            pltpu.SemaphoreType.DMA((2, size, PIECES)),
            pltpu.SemaphoreType.DMA((size, PIECES)),
            pltpu.SemaphoreType.DMA((shard_count,)),
            pltpu.SemaphoreType.DMA((shard_count,)),
        ],
        compiler_params=pltpu.CompilerParams(collective_id=0, has_side_effects=True, vmem_limit_bytes=48 << 20),
        name="project",
    )(activations, live, total, weight)


def pick(value, bit, mine, me):
    at = (me >> (bit + 1)) & 1
    return lax.dynamic_index_in_dim(value, at if mine else 1 - at, value.ndim - 3 - bit, keepdims=True)


def scatter_sum(lhs, rhs, bits, me, size):
    def times(block):
        flat = block.reshape((-1,) + block.shape[-2:])
        if flat.shape[0] == 1:
            result = contract(flat[0], rhs, ROWS)
        else:
            result = contract(flat, rhs, ((1,), (0,)))
        return result.reshape(block.shape[:-2] + (block.shape[-1], rhs.shape[1]))

    received = []
    keep = lhs
    for bit in bits:
        send = times(pick(keep, bit, False, me))
        for value in received:
            send = send + pick(value, bit, False, me).astype(F32)
        keep = pick(keep, bit, True, me)
        received = [pick(value, bit, True, me) for value in received]
        received.append(swap(send.astype(BF16), size, 2 << bit))
    total = times(keep)
    for value in received:
        total = total + value.astype(F32)
    return total.reshape(lhs.shape[-1], rhs.shape[1])


def shards(activations, qkv_weight, log_decay, lengths, out_grad):
    size = lax.axis_size("context")
    me = lax.axis_index("context")
    core = me & 1
    chip = me >> 1
    chips = size // 2
    tokens = activations.shape[0]
    heads = log_decay.shape[1]
    columns = out_grad.shape[1]
    width = columns // heads
    half = heads // 2
    scale = width ** -0.5

    token_at = jnp.arange(tokens, dtype=jnp.int32)
    live = token_at < lengths[0]
    run_sum = jnp.cumsum(log_decay * live.astype(F32)[:, None], axis=0)
    run_wide = jnp.repeat(run_sum, width, axis=1)
    run_rows = run_sum.T
    own_total = run_sum[-1].astype(BF16).astype(F32)
    total_block = jnp.broadcast_to(jnp.pad(own_total, (0, 128 - heads))[None], (8, 128))
    live_column = live.astype(F32)[:, None]
    every, q, k, v, totals = project(
        activations, qkv_weight.transpose(1, 0, 2), live_column, total_block, size, lax.axis_size("tensor")
    )
    totals = totals[:, 0, :heads]

    rows = qkv_weight.shape[0] // size
    blocks = every.shape[2] // (2 * rows)
    low_rows, high_rows = [
        jnp.stack(
            [every[:, :, (2 * at + which) * rows : (2 * at + which + 1) * rows] for at in range(blocks)], axis=1
        ).reshape(chips, tokens, rows)
        for which in (0, 1)
    ]
    own_rows = jnp.where(core == 0, low_rows, high_rows)
    other_rows = swap(jnp.where(core == 0, high_rows, low_rows), size, 1)
    lhs = jnp.concatenate([own_rows, other_rows], axis=1)

    depth = chips.bit_length() - 1
    orders = (tuple(range(depth)), tuple(reversed(range(depth))))
    lhs = lhs.reshape((2,) * depth + lhs.shape[1:])
    lefts = []
    for order in orders:
        if not depth:
            lefts.append(lhs)
            continue
        moved = swap(pick(lhs, order[0], False, me), size, 2 << order[0])
        lefts.append(jnp.concatenate([pick(lhs, order[0], True, me), moved], axis=-2))

    head_spec = pl.BlockSpec((tokens, width), lambda h: (0, h))
    square_spec = pl.BlockSpec((1, width, width), lambda h: (h, 0, 0))
    wide = lambda kind: jax.ShapeDtypeStruct((tokens, columns), kind)
    squares = jax.ShapeDtypeStruct((heads, width, width), BF16)
    state, grad_state = pl.pallas_call(
        functools.partial(states_kernel, scale),
        grid=(heads,),
        in_specs=[head_spec] * 5,
        out_specs=[square_spec] * 2,
        out_shape=[squares] * 2,
        cost_estimate=pl.CostEstimate(flops=4 * tokens * columns * width, bytes_accessed=12 * tokens * columns, transcendentals=0),
        name="states",
    )(q, k, v, out_grad, run_wide)

    both = jnp.stack([state, grad_state])
    other = swap(both, size, 1)
    mine_half = lax.dynamic_slice_in_dim(both, core * half, half, 1).astype(F32)
    other_half = lax.dynamic_slice_in_dim(other, core * half, half, 1).astype(F32)
    pair_totals = lax.dynamic_slice_in_dim(totals, chip * 2, 2, 0)
    pair_half = lax.dynamic_slice_in_dim(pair_totals, core * half, half, 1)
    low, high = [jnp.where(core == which, mine_half, other_half) for which in (0, 1)]
    chip_state = (jnp.exp(pair_half[1])[:, None, None] * low[0] + high[0]).astype(BF16)
    chip_grad = (low[1] + jnp.exp(pair_half[0])[:, None, None] * high[1]).astype(BF16)

    arrivals = [
        swap(jnp.where((chip ^ step) > chip, chip_state, chip_grad), size, 2 * step) for step in range(1, chips)
    ]

    dq, dk, dv = pl.pallas_call(
        functools.partial(intra_kernel, scale),
        grid=(heads,),
        in_specs=[head_spec] * 5 + [pl.BlockSpec((heads, tokens), lambda h: (0, 0))],
        out_specs=[head_spec] * 3,
        out_shape=[wide(F32)] * 3,
        cost_estimate=pl.CostEstimate(
            flops=10 * tokens * tokens * columns, bytes_accessed=24 * tokens * columns, transcendentals=heads * tokens * tokens
        ),
        name="intra",
    )(q, k, v, out_grad, run_wide, run_rows)

    arrivals, dq, dk, dv = lax.optimization_barrier((arrivals, dq, dk, dv))
    upto = jnp.cumsum(totals, axis=0)
    totals_half = lax.dynamic_slice_in_dim(totals, core * half, half, 1)
    upto_half = lax.dynamic_slice_in_dim(upto, core * half, half, 1)
    chip_before = lax.dynamic_index_in_dim(upto_half - totals_half, chip * 2, 0, keepdims=False)
    chip_upto = lax.dynamic_index_in_dim(upto_half, chip * 2 + 1, 0, keepdims=False)
    incoming = jnp.zeros((half, width, width), F32)
    later = jnp.zeros((half, width, width), F32)
    for step in range(1, chips):
        peer = chip ^ step
        goes_up = peer > chip
        arrived = arrivals[step - 1].astype(F32)
        peer_upto = lax.dynamic_index_in_dim(upto_half, peer * 2 + 1, 0, keepdims=False)
        peer_before = lax.dynamic_index_in_dim(upto_half - totals_half, peer * 2, 0, keepdims=False)
        gap = jnp.where(goes_up, peer_before - chip_upto, chip_before - peer_upto)
        term = jnp.exp(gap)[:, None, None] * arrived
        incoming = incoming + jnp.where(goes_up, 0.0, term)
        later = later + jnp.where(goes_up, term, 0.0)
    from_chips = jnp.stack([incoming, later]).astype(BF16)
    other_chips = swap(from_chips, size, 1)
    is_low = core == 0
    from_chips = jnp.concatenate(
        [jnp.where(is_low, from_chips, other_chips), jnp.where(is_low, other_chips, from_chips)], axis=1
    ).astype(F32)
    incoming = jnp.where(
        is_low, from_chips[0], jnp.exp(pair_totals[0])[:, None, None] * from_chips[0] + other[0].astype(F32)
    ).astype(BF16)
    later = jnp.where(
        is_low, jnp.exp(pair_totals[1])[:, None, None] * from_chips[1] + other[1].astype(F32), from_chips[1]
    ).astype(BF16)

    grads = pl.pallas_call(
        functools.partial(inter_kernel, scale),
        grid=(heads,),
        in_specs=[pl.BlockSpec(memory_space=pltpu.SMEM)] + [head_spec] * 4 + [square_spec] * 2 + [head_spec] * 3,
        out_specs=[head_spec] * 3,
        out_shape=[wide(BF16)] * 3,
        cost_estimate=pl.CostEstimate(flops=6 * tokens * columns * width, bytes_accessed=28 * tokens * columns, transcendentals=0),
        name="inter",
    )(lengths, k, v, out_grad, run_wide, incoming, later, dq, dk, dv)

    results = []
    piece = columns // 2
    for part in grads:
        halves = [part[:, :piece], part[:, piece:]]
        if depth:
            moved = [swap(value, size, 2 << order[0]) for value, order in zip(halves, orders)]
            others = swap(jnp.concatenate(moved, axis=1), size, 1)
        partner = swap(part, size, 1)
        pieces = []
        for at, order in enumerate(orders):
            columns_at = slice(at * piece, (at + 1) * piece)
            rhs = [halves[at], partner[:, columns_at]]
            if depth:
                rhs += [moved[at], others[:, columns_at]]
            pieces.append(scatter_sum(lefts[at], jnp.concatenate(rhs, axis=0), order[1:], me, size))
        results.append(jnp.concatenate(pieces, axis=1))
    return jnp.stack(results, axis=1)


def solution(mesh):
    return jax.shard_map(
        shards,
        mesh=mesh,
        in_specs=(
            P("context", "tensor"),
            P(None, None, "tensor"),
            P("context", "tensor"),
            P("context"),
            P("context", "tensor"),
        ),
        out_specs=P("context", None, "tensor"),
        check_vma=False,
    )
```
